256 devices in a mesh: users: 64 (over z, y, core), items: 4 (over x).
Axes of the slice: x: 4, y: 4, z: 8, core: 2. Of those that a mesh axis runs over, the one named last changes fastest.
Arguments:
- user_factor: bfloat16 [131072, 256], P('users'), may hold values from -2.390625 to 2.390625
- hot_factor: bfloat16 [512, 256], replicated, may hold values from -2.390625 to 2.390625
- cold_factor: bfloat16 [65536, 256], P(('users', 'items')), may hold values from -2.390625 to 2.390625
- hour_factor: bfloat16 [168, 256], replicated, may hold values from -2.390625 to 2.390625
- block_user: int32 [256, 512], P(('users', 'items')), may hold values from 0 to 2047
- block_slot: int32 [256, 512], P(('users', 'items')), may hold values from 0 to 159
- block_hour: int32 [256, 512], P(('users', 'items')), may hold values from 0 to 20
- block_count: int32 [256], P(('users', 'items')), may hold values from 128 to 512, as said below
- need_rows: int32 [256, 64, 2], P(('users', 'items')), may hold values from 0 to 15
- observed: bfloat16 [256, 512, 128], P(('users', 'items')), may hold values from 0 to 1, as said below
Outputs:
- user_grad: float32 [131072, 256], P(('users', 'items'))
- cold_grad: float32 [65536, 256], P(('users', 'items'))
- hot_grad: float32 [512, 256], P(('users', 'items'))
- hour_grad: float32 [168, 256], replicated
The draws below stay inside these ranges and needn't reach their ends.
Inputs may be any that keep to these rules, and one draw needn't show every extreme that they name: `block_count`: some device has all 512 slots live. `observed`: every entry is 0 or 1.
All inputs are finite; a program needn't handle non-finite values.
Results may differ from the reference program's by a relative error of at most 0.0029.
Values may be sent and summed in bfloat16 or wider, within the bound.
A program may use at most 128 MiB of HBM per device.

```python
import jax
import jax.numpy as jnp
from jax import lax

RANK = 256
HOURS = 168
IB = 16
HB = 8
HOT = 512
USER_DEV = 2048
ITEM_DEV = 256
REQ = 2
NBLK = 512
HOUR_BLOCKS = 21
USERS = 131072
ITEMS_COLD = 65536
SLOTS = 160
N_USERS = 64
N_ITEMS = 4


def draw_block_count(key, part):
    device_count = N_USERS * N_ITEMS
    counts = jax.random.randint(key, (device_count,), NBLK // 4, NBLK + 1)
    chosen = jax.random.randint(jax.random.fold_in(key, 7), (), 0, device_count)
    return counts.at[chosen].set(NBLK).astype(jnp.int32)


def draw_observed(key, part):
    device_count = N_USERS * N_ITEMS
    values = jax.random.bernoulli(key, 0.5, (device_count, NBLK, IB * HB)).astype(jnp.float32)
    return values.astype(jnp.bfloat16)


def touch_ends(values, stream_key, smallest, largest):
    extent = values.shape
    index_at = [jax.random.randint(jax.random.fold_in(stream_key, axis), (), 0, extent[axis]) for axis in range(len(extent))]
    values = values.at[tuple(index_at)].set(smallest)
    longest = extent.index(max(extent))
    index_at[longest] = (index_at[longest] + 1) % extent[longest]
    return values.at[tuple(index_at)].set(largest)


def block_scale(rng, extent, split, smallest, largest):
    def one(position, shards_of):
        steps = jax.random.uniform(jax.random.fold_in(jax.random.fold_in(rng, 6), position), (shards_of,), jnp.float32, smallest / len(split), largest / len(split))
        return jnp.repeat(jnp.exp(steps), extent[position] // shards_of).reshape((-1,) + (1,) * (len(extent) - position - 1))

    gain = one(*split[0])
    for cut in split[1:]:
        gain = gain * one(*cut)
    return gain


def gaussian(stream_key, dims, deviation, reach, shards=(), held_as=jnp.bfloat16):
    values = jax.random.normal(stream_key, dims, jnp.float32) * deviation
    if len(shards) > 0:
        values = block_scale(stream_key, dims, shards, -0.22, 0.18) * values
    return jnp.clip(values, min=-reach, max=reach).astype(held_as)


def setup_inputs(seed: int = 0) -> dict:
    streams_of = jax.random.split(jax.random.key(seed), 11)
    user_factor = gaussian(streams_of[0], (USERS, RANK), 0.4, 2.390625, ((0, 64),))
    hot_factor = gaussian(streams_of[1], (HOT, RANK), 0.4, 2.390625)
    cold_factor = gaussian(streams_of[2], (ITEMS_COLD, RANK), 0.4, 2.390625, ((0, 256),))
    hour_factor = gaussian(streams_of[3], (HOURS, RANK), 0.4, 2.390625)
    block_user = touch_ends(jax.random.randint(streams_of[4], (N_USERS * N_ITEMS, NBLK), 0, USER_DEV), jax.random.fold_in(streams_of[4], 1), 0, USER_DEV - 1).astype(jnp.int32)
    block_slot = touch_ends(jax.random.randint(streams_of[5], (N_USERS * N_ITEMS, NBLK), 0, SLOTS), jax.random.fold_in(streams_of[5], 1), 0, SLOTS - 1).astype(jnp.int32)
    block_hour = touch_ends(jax.random.randint(streams_of[6], (N_USERS * N_ITEMS, NBLK), 0, HOUR_BLOCKS), jax.random.fold_in(streams_of[6], 1), 0, HOUR_BLOCKS - 1).astype(jnp.int32)
    block_count = draw_block_count(jax.random.fold_in(streams_of[10], 71), 0)
    need_rows = touch_ends(jax.random.randint(streams_of[8], (N_USERS * N_ITEMS, N_USERS, REQ), 0, ITEM_DEV // IB), jax.random.fold_in(streams_of[8], 1), 0, (ITEM_DEV // IB) - 1).astype(jnp.int32)
    observed = draw_observed(jax.random.fold_in(streams_of[10], 71), 0)
    return {"user_factor": user_factor, "hot_factor": hot_factor, "cold_factor": cold_factor, "hour_factor": hour_factor, "block_user": block_user, "block_slot": block_slot, "block_hour": block_hour, "block_count": block_count, "need_rows": need_rows, "observed": observed}


def reference(user_factor, hot_factor, cold_factor, hour_factor, block_user, block_slot, block_hour, block_count, need_rows, observed):
    device_count = N_USERS * N_ITEMS
    device_ids = jnp.arange(device_count, dtype=jnp.int32)
    slab_index = device_ids // N_ITEMS
    column_index = device_ids % N_ITEMS
    hot_blocks = HOT // IB
    global_user = slab_index[:, None] * USER_DEV + block_user
    cold_slot = jnp.maximum(block_slot - hot_blocks, 0).astype(jnp.int32)
    peer_index = cold_slot // REQ
    flat_need = need_rows.reshape(device_count, N_USERS * REQ)
    picked_block = jnp.take_along_axis(flat_need, cold_slot, axis=1)
    cold_row = (peer_index * N_ITEMS + column_index[:, None]) * ITEM_DEV + picked_block * IB
    first_row = jnp.where(block_slot < hot_blocks, block_slot * IB, HOT + cold_row).astype(jnp.int32)
    live_mask = jnp.arange(NBLK, dtype=jnp.int32)[None, :] < block_count[:, None]
    group_len = min(NBLK, 512)
    total = device_count * NBLK
    groups = total // group_len
    item_table = jnp.concatenate([hot_factor, cold_factor], axis=0)
    offsets = jnp.arange(IB, dtype=jnp.int32)
    hour_offsets = jnp.arange(HB, dtype=jnp.int32)
    data = (global_user.reshape(groups, group_len), first_row.reshape(groups, group_len),
            block_hour.reshape(groups, group_len), live_mask.reshape(groups, group_len),
            observed.reshape(groups, group_len, IB, HB))

    def one_group(carry, group_data):
        grad_user, grad_item, grad_hour = carry
        users_idx, rows_idx, hours_idx, live, obs = group_data
        user_rows = user_factor[users_idx].astype(jnp.float32)
        item_idx = rows_idx[:, None] + offsets
        item_rows = item_table[item_idx].astype(jnp.float32)
        hour_rows = hour_factor[hours_idx[:, None] * HB + hour_offsets].astype(jnp.float32)
        user_item = (user_rows[:, None, :] * item_rows).astype(jnp.bfloat16)
        ui_wide = user_item.astype(jnp.float32)
        model = jnp.einsum('gar,gbr->gab', ui_wide, hour_rows)
        residual = jnp.where(live[:, None, None], jax.nn.sigmoid(model) - obs.astype(jnp.float32), 0.0).astype(jnp.bfloat16)
        res_wide = residual.astype(jnp.float32)
        weighted = jnp.einsum('gab,gbr->gar', res_wide, hour_rows)
        item_terms = weighted * user_rows[:, None, :]
        user_terms = jnp.sum(weighted * item_rows, axis=1)
        hour_terms = jnp.einsum('gab,gar->gbr', res_wide, ui_wide)
        grad_user = grad_user.at[users_idx].add(user_terms)
        grad_item = grad_item.at[item_idx.reshape(-1)].add(item_terms.reshape(-1, RANK))
        grad_hour = grad_hour.at[hours_idx].add(hour_terms.reshape(group_len, HB * RANK))
        return (grad_user, grad_item, grad_hour), None

    start = (jnp.zeros((USERS, RANK), jnp.float32), jnp.zeros((HOT + ITEMS_COLD, RANK), jnp.float32),
             jnp.zeros((HOUR_BLOCKS, HB * RANK), jnp.float32))
    (grad_user, grad_item, grad_hour), _ = lax.scan(one_group, start, data)
    return grad_user, grad_item[HOT:], grad_item[:HOT], grad_hour.reshape(HOURS, RANK)
```

```python
import functools

import jax
import jax.numpy as jnp
from jax import lax
from jax.experimental import pallas as pl
from jax.experimental.pallas import tpu as pltpu
from jax.sharding import PartitionSpec as P

IB = 16
HB = 8
REQ = 2
MESH = pl.DeviceIdType.MESH
F32 = jnp.float32
BF16 = jnp.bfloat16


def dot(a, b, ca=1, cb=0):
    return lax.dot_general(a, b, (((ca,), (cb,)), ((), ())), preferred_element_type=F32)


def onehot(mask):
    return jnp.where(mask, 1.0, 0.0).astype(BF16)


def halves(x):
    hi = x.astype(BF16)
    return hi, (x - hi.astype(F32)).astype(BF16)


def kernel(
    nu,
    ni,
    user_ref,
    hot_ref,
    cold_ref,
    hour_ref,
    bu_ref,
    bs_ref,
    bh_ref,
    cnt_ref,
    need_ref,
    obs_ref,
    ugrad_ref,
    cgrad_ref,
    hgrad_ref,
    tgrad_ref,
    idx_send,
    idx_recv,
    perm,
    row_send,
    row_recv,
    tab,
    urows,
    sel,
    sel_t,
    hours,
    obs_t,
    hour_acc,
    uterm,
    cold32,
    cold_send,
    cold_recv,
    user32,
    user_send,
    user_recv,
    xs_send,
    xs_recv,
    st2,
    st2_send,
    st2_recv,
    hall,
    hflat,
    sems,
):
    p = lax.axis_index("users")
    q = lax.axis_index("items")
    nblk = bu_ref.shape[1]
    users = user_ref.shape[0]
    udev = users // ni
    hot_rows, rank = hot_ref.shape
    cold_rows = cold_ref.shape[0]
    hot_slots = hot_rows // IB
    cold_slots = nu * REQ
    slots = hot_slots + cold_slots
    hour_count = hour_ref.shape[0]
    hour_blocks = hour_count // HB
    hp = hours.shape[0]

    def peer(i):
        h = i // 2 + 1
        return (p + h + (i % 2) * (nu - 2 * h)) % nu

    def copy_users(src, dst, n, to):
        return pltpu.make_async_remote_copy(
            src_ref=src,
            dst_ref=dst,
            send_sem=sems.at[n, 0],
            recv_sem=sems.at[n, 1],
            device_id=(to, q),
            device_id_type=MESH,
        )

    def copy_items(src, dst, n, to):
        return pltpu.make_async_remote_copy(
            src_ref=src,
            dst_ref=dst,
            send_sem=sems.at[n, 0],
            recv_sem=sems.at[n, 1],
            device_id=(p, to),
            device_id_type=MESH,
        )

    def send_users(src, dst, n, lo=0, hi=nu - 1):
        def one(i, c):
            to = peer(i)
            copy_users(src.at[to], dst.at[p], n, to).start()
            return c

        lax.fori_loop(lo, hi, one, 0)

    def wait_users(src, dst, n):
        d = copy_users(src.at[pl.ds(0, nu - 1)], dst.at[pl.ds(0, nu - 1)], n, (p + 1) % nu)
        d.wait_send()
        d.wait_recv()

    def send_items(src, dst, n, k):
        to = (q + k) % ni
        copy_items(src.at[to], dst.at[q], n, to).start()

    def wait_items(src, dst, n):
        d = copy_items(src.at[pl.ds(0, ni - 1)], dst.at[pl.ds(0, ni - 1)], n, (q + 1) % ni)
        d.wait_send()
        d.wait_recv()

    x_order = sorted(range(1, ni), key=lambda k: min(k, ni - k))

    barrier = pltpu.get_barrier_semaphore()

    def greet(i, c):
        pl.semaphore_signal(barrier, inc=1, device_id=(peer(i), q), device_id_type=MESH)
        return c

    lax.fori_loop(0, nu - 1, greet, 0)
    for k in range(1, ni):
        pl.semaphore_signal(barrier, inc=1, device_id=(p, (q + k) % ni), device_id_type=MESH)

    need = need_ref[0]
    lane = lax.broadcasted_iota(jnp.int32, (nu, 128), 1)
    wanted = jnp.where((lane // IB) % REQ == 0, need[:, 0:1], need[:, 1:2]) * IB + lane % IB + 1
    msg = jnp.where(lane // (IB * REQ) == p % 4, wanted, 0)
    for e in range(nu):
        idx_send[e] = msg[e : e + 1, :]

    for h in range(rank // 128):
        tab[h, pl.ds(0, hot_rows), :] = hot_ref[:, h * 128 : (h + 1) * 128].astype(F32)
    hours[...] = jnp.zeros_like(hours)
    hours[pl.ds(0, hour_count), :] = hour_ref[...]
    obs_t[...] = jnp.transpose(obs_ref[0].astype(F32))
    slot_col = jnp.transpose(jnp.broadcast_to(bs_ref[...], (8, nblk)))[:, 0:1]
    user_col = jnp.transpose(jnp.broadcast_to(bu_ref[...], (8, nblk)))[:, 0:1]
    sel[...] = onehot(lax.broadcasted_iota(jnp.int32, (nblk, slots), 1) == slot_col)
    sel_t[...] = onehot(lax.broadcasted_iota(jnp.int32, (slots, nblk), 0) == bs_ref[...])
    urows[...] = jnp.zeros_like(urows)

    def pick_user(c, carry):
        first = pl.multiple_of(c * 256, 256)
        mask = lax.broadcasted_iota(jnp.int32, (nblk, 256), 1) + first == user_col
        urows[...] += dot(onehot(mask), user_ref[pl.ds(first, 256), :])
        return carry

    lax.fori_loop(0, users // 256, pick_user, 0)

    pl.semaphore_wait(barrier, nu - 1 + ni - 1)

    send_users(idx_send, idx_recv, 0)
    idx_recv[pl.ds(p, 1)] = idx_send[pl.ds(p, 1)]
    uterm[...] = jnp.zeros_like(uterm)
    hour_acc[...] = jnp.zeros_like(hour_acc)
    wait_users(idx_send, idx_recv, 0)

    def build(g, c):
        v = idx_recv[4 * g] + idx_recv[4 * g + 1] + idx_recv[4 * g + 2] + idx_recv[4 * g + 3]
        m = onehot(lax.broadcasted_iota(jnp.int32, (cold_rows, 128), 0) + 1 == v)
        perm[g] = m
        rows = dot(m, cold_ref[...], 0, 0).astype(BF16)
        row_send[pl.ds(4 * g, 4)] = rows.reshape(4, IB * REQ, rank)
        return c

    lax.fori_loop(0, nu // 4, build, 0)

    send_users(row_send, row_recv, 1)
    row_recv[pl.ds(p, 1)] = row_send[pl.ds(p, 1)]
    wait_users(row_send, row_recv, 1)
    for h in range(rank // 128):
        tab[h, pl.ds(hot_rows, cold_slots * IB), :] = (
            row_recv[:, :, h * 128 : (h + 1) * 128].reshape(cold_slots * IB, 128).astype(F32)
        )

    hb = jnp.broadcast_to(bh_ref[...], (HB, nblk))
    live = lax.broadcasted_iota(jnp.int32, (HB, nblk), 1) < cnt_ref[0]

    def position(a, c):
        at = [tab[h, pl.ds(a, slots, stride=IB), :] for h in range(rank // 128)]
        items = dot(sel[...], jnp.concatenate(at, axis=1).astype(BF16))
        u = urows[...]
        ui = (u * items).astype(BF16)
        h = hours[...]
        scores = dot(h, ui, 1, 1)
        model = jnp.zeros((HB, nblk), F32)
        for k in range(hour_blocks):
            model = jnp.where(hb == k, scores[k * HB : (k + 1) * HB, :], model)
        seen = obs_t[pl.ds(pl.multiple_of(a * HB, HB), HB), :]
        residual = jnp.where(live, jax.nn.sigmoid(model) - seen, 0.0)
        pieces = [jnp.where(hb == k, residual, 0.0) for k in range(hour_blocks)]
        pieces += [jnp.zeros((HB, nblk), F32)] * (hp // HB - hour_blocks)
        spread = jnp.concatenate(pieces, axis=0).astype(BF16)
        hour_acc[pl.ds(0, hp), :] += dot(spread, ui)
        w = dot(spread, h, 0, 0)
        uterm[...] += w * items
        hi, lo = halves(w * u)
        g = dot(sel_t[...], hi) + dot(sel_t[...], lo)
        first = pl.multiple_of(((a // 8) * 2 + a % 2) * hot_slots, hot_slots)
        xs_send[(a % 8) // 2, pl.ds(first, hot_slots), :] = g[:hot_slots].astype(BF16)
        for k in range(rank // 128):
            cold32[k, pl.ds(a, cold_slots, stride=IB), :] = g[
                hot_slots:, k * 128 : (k + 1) * 128
            ]
        return c

    lax.fori_loop(0, IB, position, 0)

    per_q = rank // ni
    hot_q = hot_rows // ni
    xs_send[:, pl.ds(hot_q, per_q), :] = (
        jnp.transpose(hour_acc[...]).astype(BF16).reshape(ni, per_q, rank)
    )
    for k in range(rank // 128):
        cold_send[:, :, k * 128 : (k + 1) * 128] = (
            cold32[k].astype(BF16).reshape(nu, REQ * IB, 128)
        )
    for k in x_order:
        send_items(xs_send, xs_recv, 2, k)
    send_users(cold_send, cold_recv, 3, 0, nu // 2)

    hi, lo = halves(uterm[...])
    for c in range(ni):
        m = onehot(lax.broadcasted_iota(jnp.int32, (udev, nblk), 0) + c * udev == bu_ref[...])
        user32[c] = dot(m, hi) + dot(m, lo)
        user_send[c] = user32[c].astype(BF16)
    for k in x_order:
        send_items(user_send, user_recv, 4, k)

    xs_recv[pl.ds(q, 1)] = xs_send[pl.ds(q, 1)]
    wait_items(xs_send, xs_recv, 2)
    x1 = xs_recv[0].astype(F32)
    for k in range(1, ni):
        x1 = x1 + xs_recv[k].astype(F32)
    for half in range(2):
        for j in range(2):
            first = (half * 2 + j) * hot_slots
            for k in range(rank // 128):
                st2[j * (rank // 128) + k, pl.ds(half, hot_slots, stride=2), :] = x1[
                    first : first + hot_slots, k * 128 : (k + 1) * 128
                ]
    for k in range(rank // 128):
        st2[2 * (rank // 128) + k] = x1[hot_q : hot_q + per_q, k * 128 : (k + 1) * 128]
    for k in range(3 * rank // 128):
        for e in range(nu):
            st2_send[e, :, k * 128 : (k + 1) * 128] = st2[k, e : e + 1, :]
    send_users(st2_send, st2_recv, 5)
    send_users(cold_send, cold_recv, 3, nu // 2, nu - 1)
    st2_recv[pl.ds(p, 1)] = st2_send[pl.ds(p, 1)]
    cold_recv[pl.ds(p, 1)] = cold_send[pl.ds(p, 1)]
    wait_users(st2_send, st2_recv, 5)
    total = st2_recv[0]
    for e in range(1, nu):
        total = total + st2_recv[e]
    hgrad_ref[pl.ds(0, 1), :] = total[:, :rank]
    hgrad_ref[pl.ds(1, 1), :] = total[:, rank : 2 * rank]
    hall[q, pl.ds(p, 1)] = total[:, 2 * rank :].reshape(1, 1, rank)

    def tell(i, c):
        to = peer(i)
        copy_users(hall.at[q, p], hall.at[q, p], 6, to).start()
        return c

    lax.fori_loop(0, nu - 1, tell, 0)

    wait_items(user_send, user_recv, 4)
    user_recv[pl.ds(q, 1)] = jnp.zeros((1, udev, rank), BF16)
    grad = user32[q]
    for k in range(ni):
        grad = grad + user_recv[k].astype(F32)
    ugrad_ref[...] = grad

    wait_users(hall.at[q], hall.at[q], 6)
    for k in x_order:
        to = (q + k) % ni
        copy_items(hall.at[q], hall.at[q], 7, to).start()

    wait_users(cold_send, cold_recv, 3)
    acc = jnp.zeros((cold_rows, rank), F32)
    for g in range(nu // 4):
        acc = acc + dot(perm[g], cold_recv[pl.ds(4 * g, 4)].reshape(128, rank))
    cgrad_ref[...] = acc

    wait_items(hall, hall, 7)
    for c in range(ni):
        for e in range(nu):
            hflat[pl.ds(c * nu + e, 1), :] = hall[c, e]
    tgrad_ref[...] = jnp.transpose(hflat[...])[:hour_count, :]


def solution(mesh):
    nu, ni = mesh.shape["users"], mesh.shape["items"]

    def body(
        user_factor,
        hot_factor,
        cold_factor,
        hour_factor,
        block_user,
        block_slot,
        block_hour,
        block_count,
        need_rows,
        observed,
    ):
        users, rank = user_factor.shape
        hot_rows = hot_factor.shape[0]
        cold_rows = cold_factor.shape[0]
        hour_count = hour_factor.shape[0]
        nblk = block_user.shape[1]
        slots = hot_rows // IB + nu * REQ
        udev = users // ni
        hp = -(-hour_count // 16) * 16
        part = REQ * IB
        vmem = pl.BlockSpec(memory_space=pltpu.VMEM)
        specs = [vmem] * 10
        specs[7] = pl.BlockSpec(memory_space=pltpu.SMEM)
        small = (hot_rows + rank) // ni
        return pl.pallas_call(
            functools.partial(kernel, nu, ni),
            out_shape=(
                jax.ShapeDtypeStruct((udev, rank), F32),
                jax.ShapeDtypeStruct((cold_rows, rank), F32),
                jax.ShapeDtypeStruct((hot_rows // (nu * ni), rank), F32),
                jax.ShapeDtypeStruct((hour_count, rank), F32),
            ),
            in_specs=specs,
            out_specs=(vmem,) * 4,
            scratch_shapes=[
                pltpu.VMEM((nu, 1, 128), jnp.int32),
                pltpu.VMEM((nu, 1, 128), jnp.int32),
                pltpu.VMEM((nu // 4, cold_rows, 128), BF16),
                pltpu.VMEM((nu, part, rank), BF16),
                pltpu.VMEM((nu, part, rank), BF16),
                pltpu.VMEM((rank // 128, slots * IB, 128), F32),
                pltpu.VMEM((nblk, rank), F32),
                pltpu.VMEM((nblk, slots), BF16),
                pltpu.VMEM((slots, nblk), BF16),
                pltpu.VMEM((hp, rank), BF16),
                pltpu.VMEM((IB * HB, nblk), F32),
                pltpu.VMEM((rank, rank), F32),
                pltpu.VMEM((nblk, rank), F32),
                pltpu.VMEM((rank // 128, nu * part, 128), F32),
                pltpu.VMEM((nu, part, rank), BF16),
                pltpu.VMEM((nu, part, rank), BF16),
                pltpu.VMEM((ni, udev, rank), F32),
                pltpu.VMEM((ni, udev, rank), BF16),
                pltpu.VMEM((ni, udev, rank), BF16),
                pltpu.VMEM((ni, small, rank), BF16),
                pltpu.VMEM((ni, small, rank), BF16),
                pltpu.VMEM((3 * rank // 128, nu, 128), F32),
                pltpu.VMEM((nu, 1, 3 * rank), F32),
                pltpu.VMEM((nu, 1, 3 * rank), F32),
                pltpu.VMEM((ni, nu, 1, rank), F32),
                pltpu.VMEM((rank, rank), F32),
                pltpu.SemaphoreType.DMA((8, 2)),
            ],
            compiler_params=pltpu.CompilerParams(
                collective_id=0, has_side_effects=True, vmem_limit_bytes=56 * 1024 * 1024
            ),
        )(
            user_factor,
            hot_factor,
            cold_factor,
            hour_factor,
            block_user,
            block_slot,
            block_hour,
            block_count,
            need_rows,
            observed,
        )

    in_specs = (
        P("users", None),
        P(),
        P(("users", "items"), None),
        P(),
        P(("users", "items"), None),
        P(("users", "items"), None),
        P(("users", "items"), None),
        P(("users", "items")),
        P(("users", "items"), None, None),
        P(("users", "items"), None, None),
    )
    out_specs = (
        P(("users", "items"), None),
        P(("users", "items"), None),
        P(("users", "items"), None),
        P(),
    )
    return jax.shard_map(body, mesh=mesh, in_specs=in_specs, out_specs=out_specs, check_vma=False)
```

```python
import functools

import jax
import jax.numpy as jnp
from jax import lax
from jax.experimental import pallas as pl
from jax.experimental.pallas import tpu as pltpu
from jax.sharding import PartitionSpec as P

IB = 16
HB = 8
REQ = 2
CH = 4
POS = IB // CH
EARLY = 2
ROWS = REQ * POS
MESH = pl.DeviceIdType.MESH
F32 = jnp.float32
BF16 = jnp.bfloat16


def dot(a, b, ca=1, cb=0):
    return lax.dot_general(a, b, (((ca,), (cb,)), ((), ())), preferred_element_type=F32)


def onehot(mask):
    return jnp.where(mask, 1.0, 0.0).astype(BF16)


def halves(x):
    hi = x.astype(BF16)
    return hi, (x - hi.astype(F32)).astype(BF16)


def kernel(
    nu,
    ni,
    user_ref,
    hot_ref,
    cold_ref,
    hour_ref,
    bu_ref,
    bs_ref,
    bh_ref,
    cnt_ref,
    need_ref,
    obs_ref,
    ugrad_ref,
    cgrad_ref,
    hgrad_ref,
    tgrad_ref,
    idx_send,
    idx_recv,
    perm,
    row_send,
    row_recv,
    hot_tab,
    tab,
    urows,
    sel,
    sel_t,
    hours,
    obs_t,
    hour_acc,
    uterm,
    cold32,
    cold_send,
    cold_recv,
    user32,
    user_send,
    user_recv,
    xs_send,
    xs_recv,
    st2,
    st2_send,
    st2_recv,
    hall,
    hflat,
    sems,
):
    p = lax.axis_index("users")
    q = lax.axis_index("items")
    nblk = bu_ref.shape[1]
    users = user_ref.shape[0]
    udev = users // ni
    hot_rows, rank = hot_ref.shape
    cold_rows = cold_ref.shape[0]
    hot_slots = hot_rows // IB
    cold_slots = nu * REQ
    slots = hot_slots + cold_slots
    hour_count = hour_ref.shape[0]
    hour_blocks = hour_count // HB
    hp = hours.shape[0]

    def peer(i):
        h = i // 2 + 1
        return (p + h + (i % 2) * (nu - 2 * h)) % nu

    def copy_users(src, dst, n, to):
        return pltpu.make_async_remote_copy(
            src_ref=src,
            dst_ref=dst,
            send_sem=sems.at[n, 0],
            recv_sem=sems.at[n, 1],
            device_id=(to, q),
            device_id_type=MESH,
        )

    def copy_items(src, dst, n, to):
        return pltpu.make_async_remote_copy(
            src_ref=src,
            dst_ref=dst,
            send_sem=sems.at[n, 0],
            recv_sem=sems.at[n, 1],
            device_id=(p, to),
            device_id_type=MESH,
        )

    def send_users(src, dst, n, lo=0, hi=nu - 1):
        def one(i, c):
            to = peer(i)
            copy_users(src.at[to], dst.at[p], n, to).start()
            return c

        lax.fori_loop(lo, hi, one, 0)

    def wait_users(src, dst, n):
        d = copy_users(src.at[pl.ds(0, nu - 1)], dst.at[pl.ds(0, nu - 1)], n, (p + 1) % nu)
        d.wait_send()
        d.wait_recv()

    def send_items(src, dst, n, k):
        to = (q + k) % ni
        copy_items(src.at[to], dst.at[q], n, to).start()

    def wait_items(src, dst, n):
        d = copy_items(src.at[pl.ds(0, ni - 1)], dst.at[pl.ds(0, ni - 1)], n, (q + 1) % ni)
        d.wait_send()
        d.wait_recv()

    x_order = sorted(range(1, ni), key=lambda k: min(k, ni - k))

    barrier = pltpu.get_barrier_semaphore()

    def greet(i, c):
        pl.semaphore_signal(barrier, inc=1, device_id=(peer(i), q), device_id_type=MESH)
        return c

    lax.fori_loop(0, nu - 1, greet, 0)
    for k in range(1, ni):
        pl.semaphore_signal(barrier, inc=1, device_id=(p, (q + k) % ni), device_id_type=MESH)

    span = 128 // ROWS
    need = need_ref[0]
    lane = lax.broadcasted_iota(jnp.int32, (nu, 128), 1)
    wanted = jnp.where((lane // POS) % REQ == 0, need[:, 0:1], need[:, 1:2]) * IB + lane % POS + 1
    msg = jnp.where(lane // ROWS == p % span, wanted, 0)
    for e in range(nu):
        idx_send[e] = msg[e : e + 1, :]

    for h in range(rank // 128):
        hot_tab[h] = hot_ref[:, h * 128 : (h + 1) * 128].astype(F32)
    hours[...] = jnp.zeros_like(hours)
    hours[pl.ds(0, hour_count), :] = hour_ref[...]
    obs_t[...] = jnp.transpose(obs_ref[0].astype(F32))
    slot_col = jnp.transpose(jnp.broadcast_to(bs_ref[...], (8, nblk)))[:, 0:1]
    user_col = jnp.transpose(jnp.broadcast_to(bu_ref[...], (8, nblk)))[:, 0:1]
    sel[...] = onehot(lax.broadcasted_iota(jnp.int32, (nblk, slots), 1) == slot_col)
    sel_t[...] = onehot(lax.broadcasted_iota(jnp.int32, (slots, nblk), 0) == bs_ref[...])
    urows[...] = jnp.zeros_like(urows)

    def pick_user(c, carry):
        first = pl.multiple_of(c * 256, 256)
        mask = lax.broadcasted_iota(jnp.int32, (nblk, 256), 1) + first == user_col
        urows[...] += dot(onehot(mask), user_ref[pl.ds(first, 256), :])
        return carry

    lax.fori_loop(0, users // 256, pick_user, 0)

    pl.semaphore_wait(barrier, nu - 1 + ni - 1)

    send_users(idx_send, idx_recv, 0)
    idx_recv[pl.ds(p, 1)] = idx_send[pl.ds(p, 1)]
    uterm[...] = jnp.zeros_like(uterm)
    hour_acc[...] = jnp.zeros_like(hour_acc)
    wait_users(idx_send, idx_recv, 0)

    groups = nu // span

    def build(i, carry):
        c = i // groups
        g = i % groups
        first = pl.multiple_of(g * span, span)
        v = jnp.sum(idx_recv[pl.ds(first, span)], axis=0) - 1 + c * POS
        m = onehot(lax.broadcasted_iota(jnp.int32, (cold_rows, 128), 0) == v)
        perm[i] = m
        rows = dot(m, cold_ref[...], 0, 0).astype(BF16)
        row_send[c, pl.ds(first, span)] = rows.reshape(span, ROWS, rank)
        return carry

    def build_and_send(c, carry):
        lax.fori_loop(c * groups, (c + 1) * groups, build, 0)
        send_users(row_send.at[c], row_recv.at[c], 8 + c)
        row_recv[c, pl.ds(p, 1)] = row_send[c, pl.ds(p, 1)]
        return carry

    lax.fori_loop(0, CH, build_and_send, 0)

    hb = jnp.broadcast_to(bh_ref[...], (HB, nblk))
    live = lax.broadcasted_iota(jnp.int32, (HB, nblk), 1) < cnt_ref[0]

    def position(a, carry):
        at = [
            jnp.concatenate(
                [
                    hot_tab[h, pl.ds(a, hot_slots, stride=IB), :],
                    tab[h, pl.ds(a % POS, cold_slots, stride=POS), :],
                ],
                axis=0,
            )
            for h in range(rank // 128)
        ]
        items = dot(sel[...], jnp.concatenate(at, axis=1).astype(BF16))
        u = urows[...]
        ui = (u * items).astype(BF16)
        h = hours[...]
        scores = dot(h, ui, 1, 1)
        model = jnp.zeros((HB, nblk), F32)
        for k in range(hour_blocks):
            model = jnp.where(hb == k, scores[k * HB : (k + 1) * HB, :], model)
        seen = obs_t[pl.ds(pl.multiple_of(a * HB, HB), HB), :]
        residual = jnp.where(live, jax.nn.sigmoid(model) - seen, 0.0)
        pieces = [jnp.where(hb == k, residual, 0.0) for k in range(hour_blocks)]
        pieces += [jnp.zeros((HB, nblk), F32)] * (hp // HB - hour_blocks)
        spread = jnp.concatenate(pieces, axis=0).astype(BF16)
        hour_acc[pl.ds(0, hp), :] += dot(spread, ui)
        w = dot(spread, h, 0, 0)
        uterm[...] += w * items
        hi, lo = halves(w * u)
        g = dot(sel_t[...], hi) + dot(sel_t[...], lo)
        first = pl.multiple_of(((a // 8) * 2 + a % 2) * hot_slots, hot_slots)
        xs_send[(a % 8) // 2, pl.ds(first, hot_slots), :] = g[:hot_slots].astype(BF16)
        for k in range(rank // 128):
            cold32[k, pl.ds(a % POS, cold_slots, stride=POS), :] = g[
                hot_slots:, k * 128 : (k + 1) * 128
            ]
        return carry

    def chunk(c, carry):
        wait_users(row_send.at[c], row_recv.at[c], 8 + c)
        for h in range(rank // 128):
            tab[h] = row_recv[c, :, :, h * 128 : (h + 1) * 128].astype(F32).reshape(-1, 128)
        lax.fori_loop(c * POS, (c + 1) * POS, position, 0)
        for k in range(rank // 128):
            cold_send[c, :, :, k * 128 : (k + 1) * 128] = (
                cold32[k].reshape(nu, ROWS, 128).astype(BF16)
            )
        cold_recv[c, pl.ds(p, 1)] = cold_send[c, pl.ds(p, 1)]

        @pl.when(c < EARLY)
        def _():
            send_cold(c)

        return carry

    def send_cold(c):
        send_users(cold_send.at[c], cold_recv.at[c], 8 + CH + c)

    lax.fori_loop(0, CH, chunk, 0)

    per_q = rank // ni
    hot_q = hot_rows // ni
    xs_send[:, pl.ds(hot_q, per_q), :] = (
        jnp.transpose(hour_acc[...]).astype(BF16).reshape(ni, per_q, rank)
    )
    for k in x_order:
        send_items(xs_send, xs_recv, 2, k)

    hi, lo = halves(uterm[...])
    for c in range(ni):
        m = onehot(lax.broadcasted_iota(jnp.int32, (udev, nblk), 0) + c * udev == bu_ref[...])
        user32[c] = dot(m, hi) + dot(m, lo)
        user_send[c] = user32[c].astype(BF16)
    for k in x_order:
        send_items(user_send, user_recv, 4, k)

    xs_recv[pl.ds(q, 1)] = xs_send[pl.ds(q, 1)]
    wait_items(xs_send, xs_recv, 2)
    x1 = xs_recv[0].astype(F32)
    for k in range(1, ni):
        x1 = x1 + xs_recv[k].astype(F32)
    for half in range(2):
        for j in range(2):
            first = (half * 2 + j) * hot_slots
            for k in range(rank // 128):
                st2[j * (rank // 128) + k, pl.ds(half, hot_slots, stride=2), :] = x1[
                    first : first + hot_slots, k * 128 : (k + 1) * 128
                ]
    for k in range(rank // 128):
        st2[2 * (rank // 128) + k] = x1[hot_q : hot_q + per_q, k * 128 : (k + 1) * 128]
    for k in range(3 * rank // 128):
        for e in range(nu):
            st2_send[e, :, k * 128 : (k + 1) * 128] = st2[k, e : e + 1, :]
    send_users(st2_send, st2_recv, 5)
    for c in range(EARLY, CH - 1):
        send_cold(c)
    st2_recv[pl.ds(p, 1)] = st2_send[pl.ds(p, 1)]
    wait_users(st2_send, st2_recv, 5)
    total = st2_recv[0]
    for e in range(1, nu):
        total = total + st2_recv[e]
    hgrad_ref[pl.ds(0, 1), :] = total[:, :rank]
    hgrad_ref[pl.ds(1, 1), :] = total[:, rank : 2 * rank]
    hall[q, pl.ds(p, 1)] = total[:, 2 * rank :].reshape(1, 1, rank)

    def tell(i, c):
        to = peer(i)
        copy_users(hall.at[q, p], hall.at[q, p], 6, to).start()
        return c

    lax.fori_loop(0, nu - 1, tell, 0)
    if EARLY < CH:
        send_cold(CH - 1)

    wait_items(user_send, user_recv, 4)
    user_recv[pl.ds(q, 1)] = jnp.zeros((1, udev, rank), BF16)
    grad = user32[q]
    for k in range(ni):
        grad = grad + user_recv[k].astype(F32)
    ugrad_ref[...] = grad

    wait_users(hall.at[q], hall.at[q], 6)
    for k in x_order:
        to = (q + k) % ni
        copy_items(hall.at[q], hall.at[q], 7, to).start()

    cgrad_ref[...] = jnp.zeros_like(cgrad_ref)

    def collect(c, carry):
        wait_users(cold_send.at[c], cold_recv.at[c], 8 + CH + c)
        acc = cgrad_ref[...]
        for g in range(groups):
            part = cold_recv[c, pl.ds(span * g, span)].reshape(128, rank)
            acc = acc + dot(perm[c * groups + g], part)
        cgrad_ref[...] = acc
        return carry

    lax.fori_loop(0, CH, collect, 0)

    wait_items(hall, hall, 7)
    for c in range(ni):
        for e in range(nu):
            hflat[pl.ds(c * nu + e, 1), :] = hall[c, e]
    tgrad_ref[...] = jnp.transpose(hflat[...])[:hour_count, :]


def solution(mesh):
    nu, ni = mesh.shape["users"], mesh.shape["items"]

    def body(
        user_factor,
        hot_factor,
        cold_factor,
        hour_factor,
        block_user,
        block_slot,
        block_hour,
        block_count,
        need_rows,
        observed,
    ):
        users, rank = user_factor.shape
        hot_rows = hot_factor.shape[0]
        cold_rows = cold_factor.shape[0]
        hour_count = hour_factor.shape[0]
        nblk = block_user.shape[1]
        slots = hot_rows // IB + nu * REQ
        udev = users // ni
        hp = -(-hour_count // 16) * 16
        part = REQ * IB
        vmem = pl.BlockSpec(memory_space=pltpu.VMEM)
        specs = [vmem] * 10
        specs[7] = pl.BlockSpec(memory_space=pltpu.SMEM)
        small = (hot_rows + rank) // ni
        return pl.pallas_call(
            functools.partial(kernel, nu, ni),
            out_shape=(
                jax.ShapeDtypeStruct((udev, rank), F32),
                jax.ShapeDtypeStruct((cold_rows, rank), F32),
                jax.ShapeDtypeStruct((hot_rows // (nu * ni), rank), F32),
                jax.ShapeDtypeStruct((hour_count, rank), F32),
            ),
            in_specs=specs,
            out_specs=(vmem,) * 4,
            scratch_shapes=[
                pltpu.VMEM((nu, 1, 128), jnp.int32),
                pltpu.VMEM((nu, 1, 128), jnp.int32),
                pltpu.VMEM((nu * part // 128, cold_rows, 128), BF16),
                pltpu.VMEM((CH, nu, ROWS, rank), BF16),
                pltpu.VMEM((CH, nu, ROWS, rank), BF16),
                pltpu.VMEM((rank // 128, hot_rows, 128), F32),
                pltpu.VMEM((rank // 128, nu * ROWS, 128), F32),
                pltpu.VMEM((nblk, rank), F32),
                pltpu.VMEM((nblk, slots), BF16),
                pltpu.VMEM((slots, nblk), BF16),
                pltpu.VMEM((hp, rank), BF16),
                pltpu.VMEM((IB * HB, nblk), F32),
                pltpu.VMEM((rank, rank), F32),
                pltpu.VMEM((nblk, rank), F32),
                pltpu.VMEM((rank // 128, nu * ROWS, 128), F32),
                pltpu.VMEM((CH, nu, ROWS, rank), BF16),
                pltpu.VMEM((CH, nu, ROWS, rank), BF16),
                pltpu.VMEM((ni, udev, rank), F32),
                pltpu.VMEM((ni, udev, rank), BF16),
                pltpu.VMEM((ni, udev, rank), BF16),
                pltpu.VMEM((ni, small, rank), BF16),
                pltpu.VMEM((ni, small, rank), BF16),
                pltpu.VMEM((3 * rank // 128, nu, 128), F32),
                pltpu.VMEM((nu, 1, 3 * rank), F32),
                pltpu.VMEM((nu, 1, 3 * rank), F32),
                pltpu.VMEM((ni, nu, 1, rank), F32),
                pltpu.VMEM((rank, rank), F32),
                pltpu.SemaphoreType.DMA((8 + 2 * CH, 2)),
            ],
            compiler_params=pltpu.CompilerParams(
                collective_id=0, has_side_effects=True, vmem_limit_bytes=56 * 1024 * 1024
            ),
        )(
            user_factor,
            hot_factor,
            cold_factor,
            hour_factor,
            block_user,
            block_slot,
            block_hour,
            block_count,
            need_rows,
            observed,
        )

    in_specs = (
        P("users", None),
        P(),
        P(("users", "items"), None),
        P(),
        P(("users", "items"), None),
        P(("users", "items"), None),
        P(("users", "items"), None),
        P(("users", "items")),
        P(("users", "items"), None, None),
        P(("users", "items"), None, None),
    )
    out_specs = (
        P(("users", "items"), None),
        P(("users", "items"), None),
        P(("users", "items"), None),
        P(),
    )
    return jax.shard_map(body, mesh=mesh, in_specs=in_specs, out_specs=out_specs, check_vma=False)
```

```python
import functools

import jax
import jax.numpy as jnp
from jax import lax
from jax.experimental import pallas as pl
from jax.experimental.pallas import tpu as pltpu
from jax.sharding import PartitionSpec as P

IB = 16
HB = 8
REQ = 2
CH = 4
POS = IB // CH
EARLY = 3
UNROLL = 9
ROWS = REQ * POS
MESH = pl.DeviceIdType.MESH
F32 = jnp.float32
BF16 = jnp.bfloat16


def dot(a, b, ca=1, cb=0):
    return lax.dot_general(a, b, (((ca,), (cb,)), ((), ())), preferred_element_type=F32)


def onehot(mask):
    return jnp.where(mask, 1.0, 0.0).astype(BF16)


def halves(x):
    hi = x.astype(BF16)
    return hi, (x - hi.astype(F32)).astype(BF16)


def kernel(
    nu,
    ni,
    user_ref,
    hot_ref,
    cold_ref,
    hour_ref,
    bu_ref,
    bs_ref,
    bh_ref,
    cnt_ref,
    need_ref,
    obs_ref,
    ugrad_ref,
    cgrad_ref,
    hgrad_ref,
    tgrad_ref,
    idx_send,
    idx_recv,
    perm,
    row_send,
    row_recv,
    hot_tab,
    tab,
    urows,
    sel,
    sel_t,
    hours,
    obs_t,
    hour_acc,
    uterm,
    cold32,
    cold_send,
    cold_recv,
    user32,
    user_send,
    user_recv,
    sel_u,
    hot_send,
    hot_recv,
    hour_send,
    hour_recv,
    hrow_send,
    hrow_recv,
    st2,
    st2_send,
    st2_recv,
    hall,
    hflat,
    sems,
):
    p = lax.axis_index("users")
    q = lax.axis_index("items")
    nblk = bu_ref.shape[1]
    users = user_ref.shape[0]
    udev = users // ni
    hot_rows, rank = hot_ref.shape
    cold_rows = cold_ref.shape[0]
    hot_slots = hot_rows // IB
    cold_slots = nu * REQ
    slots = hot_slots + cold_slots
    hour_count = hour_ref.shape[0]
    hour_blocks = hour_count // HB
    hp = hours.shape[0]

    def each_peer(act):
        def some(i, c):
            for j in range(UNROLL):
                to = p + 1 + i * UNROLL + j
                act(jnp.where(to >= nu, to - nu, to))
            return c

        steps = (nu - 1) // UNROLL
        lax.fori_loop(0, steps, some, 0)
        for j in range(steps * UNROLL, nu - 1):
            to = p + 1 + j
            act(jnp.where(to >= nu, to - nu, to))

    def copy_users(src, dst, n, to):
        return pltpu.make_async_remote_copy(
            src_ref=src,
            dst_ref=dst,
            send_sem=sems.at[n, 0],
            recv_sem=sems.at[n, 1],
            device_id=(to, q),
            device_id_type=MESH,
        )

    def copy_items(src, dst, n, to):
        return pltpu.make_async_remote_copy(
            src_ref=src,
            dst_ref=dst,
            send_sem=sems.at[n, 0],
            recv_sem=sems.at[n, 1],
            device_id=(p, to),
            device_id_type=MESH,
        )

    def send_users(src, dst, n):
        each_peer(lambda to: copy_users(src.at[to], dst.at[p], n, to).start())

    def wait_users(src, dst, n):
        d = copy_users(src.at[pl.ds(0, nu - 1)], dst.at[pl.ds(0, nu - 1)], n, (p + 1) % nu)
        d.wait_send()
        d.wait_recv()

    def send_items(src, dst, n, k):
        to = (q + k) % ni
        copy_items(src.at[to], dst.at[q], n, to).start()

    def wait_items(src, dst, n):
        d = copy_items(src.at[pl.ds(0, ni - 1)], dst.at[pl.ds(0, ni - 1)], n, (q + 1) % ni)
        d.wait_send()
        d.wait_recv()

    x_order = sorted(range(1, ni), key=lambda k: min(k, ni - k))

    barrier = pltpu.get_barrier_semaphore()

    each_peer(
        lambda to: pl.semaphore_signal(barrier, inc=1, device_id=(to, q), device_id_type=MESH)
    )
    for k in range(1, ni):
        pl.semaphore_signal(barrier, inc=1, device_id=(p, (q + k) % ni), device_id_type=MESH)

    span = 128 // ROWS
    need = need_ref[0]
    lane = lax.broadcasted_iota(jnp.int32, (nu, 128), 1)
    wanted = jnp.where((lane // POS) % REQ == 0, need[:, 0:1], need[:, 1:2]) * IB + lane % POS + 1
    msg = jnp.where(lane // ROWS == p % span, wanted, 0)
    for e in range(nu):
        idx_send[e] = msg[e : e + 1, :]

    for h in range(rank // 128):
        hot_tab[h] = hot_ref[:, h * 128 : (h + 1) * 128].astype(F32)
    hours[...] = jnp.zeros_like(hours)
    hours[pl.ds(0, hour_count), :] = hour_ref[...]
    obs_t[...] = jnp.transpose(obs_ref[0].astype(F32))
    slot_col = jnp.transpose(jnp.broadcast_to(bs_ref[...], (8, nblk)))[:, 0:1]
    user_col = jnp.transpose(jnp.broadcast_to(bu_ref[...], (8, nblk)))[:, 0:1]
    sel[...] = onehot(lax.broadcasted_iota(jnp.int32, (nblk, slots), 1) == slot_col)
    sel_t[...] = onehot(lax.broadcasted_iota(jnp.int32, (slots, nblk), 0) == bs_ref[...])
    for c in range(ni):
        sel_u[c] = onehot(
            lax.broadcasted_iota(jnp.int32, (udev, nblk), 0) + c * udev == bu_ref[...]
        )
    urows[...] = jnp.zeros_like(urows)

    def pick_user(c, carry):
        first = pl.multiple_of(c * 256, 256)
        mask = lax.broadcasted_iota(jnp.int32, (nblk, 256), 1) + first == user_col
        urows[...] += dot(onehot(mask), user_ref[pl.ds(first, 256), :])
        return carry

    lax.fori_loop(0, users // 256, pick_user, 0)

    pl.semaphore_wait(barrier, nu - 1 + ni - 1)

    send_users(idx_send, idx_recv, 0)
    idx_recv[pl.ds(p, 1)] = idx_send[pl.ds(p, 1)]
    uterm[...] = jnp.zeros_like(uterm)
    hour_acc[...] = jnp.zeros_like(hour_acc)
    wait_users(idx_send, idx_recv, 0)

    groups = nu // span

    def build(i, carry):
        c = i // groups
        g = i % groups
        first = pl.multiple_of(g * span, span)
        v = jnp.sum(idx_recv[pl.ds(first, span)], axis=0) - 1 + c * POS
        m = onehot(lax.broadcasted_iota(jnp.int32, (cold_rows, 128), 0) == v)
        perm[i] = m
        rows = dot(m, cold_ref[...], 0, 0).astype(BF16)
        row_send[c, pl.ds(first, span)] = rows.reshape(span, ROWS, rank)
        return carry

    def build_and_send(c, carry):
        lax.fori_loop(c * groups, (c + 1) * groups, build, 0)
        send_users(row_send.at[c], row_recv.at[c], 8 + c)
        row_recv[c, pl.ds(p, 1)] = row_send[c, pl.ds(p, 1)]
        return carry

    lax.fori_loop(0, CH, build_and_send, 0)

    hb = jnp.broadcast_to(bh_ref[...], (HB, nblk))
    live = lax.broadcasted_iota(jnp.int32, (HB, nblk), 1) < cnt_ref[0]

    def position(a, carry):
        at = [
            jnp.concatenate(
                [
                    hot_tab[h, pl.ds(a, hot_slots, stride=IB), :],
                    tab[h, pl.ds(a % POS, cold_slots, stride=POS), :],
                ],
                axis=0,
            )
            for h in range(rank // 128)
        ]
        items = dot(sel[...], jnp.concatenate(at, axis=1).astype(BF16))
        u = urows[...]
        ui = (u * items).astype(BF16)
        h = hours[...]
        scores = dot(h, ui, 1, 1)
        model = jnp.zeros((HB, nblk), F32)
        for k in range(hour_blocks):
            model = jnp.where(hb == k, scores[k * HB : (k + 1) * HB, :], model)
        seen = obs_t[pl.ds(pl.multiple_of(a * HB, HB), HB), :]
        residual = jnp.where(live, jax.nn.sigmoid(model) - seen, 0.0)
        pieces = [jnp.where(hb == k, residual, 0.0) for k in range(hour_blocks)]
        pieces += [jnp.zeros((HB, nblk), F32)] * (hp // HB - hour_blocks)
        spread = jnp.concatenate(pieces, axis=0).astype(BF16)
        hour_acc[pl.ds(0, hp), :] += dot(spread, ui)
        w = dot(spread, h, 0, 0)
        uterm[...] += w * items
        hi, lo = halves(w * u)
        g = dot(sel_t[...], hi) + dot(sel_t[...], lo)
        first = pl.multiple_of((a % 2) * hot_slots, hot_slots)
        hot_send[a // POS, (a % POS) // 2, pl.ds(first, hot_slots), :] = g[:hot_slots].astype(BF16)
        for k in range(rank // 128):
            cold32[k, pl.ds(a % POS, cold_slots, stride=POS), :] = g[
                hot_slots:, k * 128 : (k + 1) * 128
            ]
        return carry

    def chunk(c, carry):
        wait_users(row_send.at[c], row_recv.at[c], 8 + c)
        for h in range(rank // 128):
            tab[h] = row_recv[c, :, :, h * 128 : (h + 1) * 128].astype(F32).reshape(-1, 128)
        lax.fori_loop(c * POS, (c + 1) * POS, position, 0)
        for k in range(rank // 128):
            cold_send[c, :, :, k * 128 : (k + 1) * 128] = (
                cold32[k].reshape(nu, ROWS, 128).astype(BF16)
            )
        cold_recv[c, pl.ds(p, 1)] = cold_send[c, pl.ds(p, 1)]

        @pl.when(c < EARLY)
        def _():
            send_cold(c)

        half = c // 2
        for i in range(2):
            to = 2 * (c % 2) + i

            @pl.when(to != q)
            def _():
                copy_items(hot_send.at[c, i], hot_recv.at[half, q], 2 + half, to).start()

            @pl.when(to == q)
            def _():
                hot_recv[half, pl.ds(q, 1)] = hot_send[c, pl.ds(i, 1)]

        return carry

    def send_cold(c):
        send_users(cold_send.at[c], cold_recv.at[c], 8 + CH + c)

    lax.fori_loop(0, CH, chunk, 0)

    per_q = rank // ni
    halves_of = rank // 128
    hour_send[...] = jnp.transpose(hour_acc[...]).astype(BF16).reshape(ni, per_q, rank)
    for k in x_order:
        send_items(hour_send, hour_recv, 6, k)
    hour_recv[pl.ds(q, 1)] = hour_send[pl.ds(q, 1)]

    hi, lo = halves(uterm[...])
    for c in range(ni):
        m = sel_u[c]
        user32[c] = dot(m, hi) + dot(m, lo)
        user_send[c] = user32[c].astype(BF16)
    for k in x_order:
        send_items(user_send, user_recv, 4, k)

    wait_items(hour_send, hour_recv, 6)
    x1 = hour_recv[0].astype(F32)
    for k in range(1, ni):
        x1 = x1 + hour_recv[k].astype(F32)
    for e in range(nu):
        hrow_send[e] = x1[e : e + 1, :]
    send_users(hrow_send, hrow_recv, 1)
    hrow_recv[pl.ds(p, 1)] = hrow_send[pl.ds(p, 1)]
    for c in range(EARLY, CH):
        send_cold(c)

    for half in range(2):
        d = copy_items(
            hot_recv.at[half, pl.ds(0, ni - 1)],
            hot_recv.at[half, pl.ds(0, ni - 1)],
            2 + half,
            (q + 1) % ni,
        )
        d.wait_send()
        d.wait_recv()
        x1 = hot_recv[half, 0].astype(F32)
        for k in range(1, ni):
            x1 = x1 + hot_recv[half, k].astype(F32)
        for j in range(2):
            for k in range(halves_of):
                st2[j * halves_of + k, pl.ds(half, hot_slots, stride=2), :] = x1[
                    j * hot_slots : (j + 1) * hot_slots, k * 128 : (k + 1) * 128
                ]
    for k in range(2 * halves_of):
        for e in range(nu):
            st2_send[e, :, k * 128 : (k + 1) * 128] = st2[k, e : e + 1, :]

    wait_users(hrow_send, hrow_recv, 1)
    total = hrow_recv[0]
    for e in range(1, nu):
        total = total + hrow_recv[e]
    hall[q, pl.ds(p, 1)] = total.reshape(1, 1, rank)

    mine = hall.at[q, p]
    each_peer(lambda to: copy_users(mine, mine, 7, to).start())
    send_users(st2_send, st2_recv, 5)
    st2_recv[pl.ds(p, 1)] = st2_send[pl.ds(p, 1)]

    cgrad_ref[...] = jnp.zeros_like(cgrad_ref)

    def collect(c, carry):
        wait_users(cold_send.at[c], cold_recv.at[c], 8 + CH + c)
        acc = cgrad_ref[...]
        for g in range(groups):
            part = cold_recv[c, pl.ds(span * g, span)].reshape(128, rank)
            acc = acc + dot(perm[c * groups + g], part)
        cgrad_ref[...] = acc
        return carry

    lax.fori_loop(0, CH - 1, collect, 0)

    wait_users(hall.at[q], hall.at[q], 7)
    for k in x_order:
        to = (q + k) % ni
        copy_items(hall.at[q], hall.at[q], 8 + 2 * CH, to).start()

    collect(CH - 1, 0)
    wait_users(st2_send, st2_recv, 5)
    total = st2_recv[0]
    for e in range(1, nu):
        total = total + st2_recv[e]
    hgrad_ref[pl.ds(0, 1), :] = total[:, :rank]
    hgrad_ref[pl.ds(1, 1), :] = total[:, rank : 2 * rank]

    wait_items(user_send, user_recv, 4)
    user_recv[pl.ds(q, 1)] = jnp.zeros((1, udev, rank), BF16)
    grad = user32[q]
    for k in range(ni):
        grad = grad + user_recv[k].astype(F32)
    ugrad_ref[...] = grad

    wait_items(hall, hall, 8 + 2 * CH)
    for c in range(ni):
        for e in range(nu):
            hflat[pl.ds(c * nu + e, 1), :] = hall[c, e]
    tgrad_ref[...] = jnp.transpose(hflat[...])[:hour_count, :]


def keep(*refs):
    src, dst, buf, sems = refs[:4], refs[4:8], refs[8:12], refs[12]
    loads = [pltpu.make_async_copy(src[i], buf[i], sems.at[i, 0]) for i in range(4)]
    stores = [pltpu.make_async_copy(buf[i], dst[i], sems.at[i, 1]) for i in range(4)]
    for load in loads:
        load.start()
    for load, store in zip(loads, stores):
        load.wait()
        store.start()
    for store in stores:
        store.wait()


def solution(mesh):
    nu, ni = mesh.shape["users"], mesh.shape["items"]

    def body(
        user_factor,
        hot_factor,
        cold_factor,
        hour_factor,
        block_user,
        block_slot,
        block_hour,
        block_count,
        need_rows,
        observed,
    ):
        users, rank = user_factor.shape
        hot_rows = hot_factor.shape[0]
        cold_rows = cold_factor.shape[0]
        hour_count = hour_factor.shape[0]
        nblk = block_user.shape[1]
        slots = hot_rows // IB + nu * REQ
        udev = users // ni
        hp = -(-hour_count // 16) * 16
        part = REQ * IB
        vmem = pl.BlockSpec(memory_space=pltpu.VMEM)
        specs = [vmem] * 10
        specs[7] = pl.BlockSpec(memory_space=pltpu.SMEM)
        results = pl.pallas_call(
            functools.partial(kernel, nu, ni),
            out_shape=(
                jax.ShapeDtypeStruct((udev, rank), F32),
                jax.ShapeDtypeStruct((cold_rows, rank), F32),
                jax.ShapeDtypeStruct((hot_rows // (nu * ni), rank), F32),
                jax.ShapeDtypeStruct((hour_count, rank), F32),
            ),
            in_specs=specs,
            out_specs=(vmem,) * 4,
            scratch_shapes=[
                pltpu.VMEM((nu, 1, 128), jnp.int32),
                pltpu.VMEM((nu, 1, 128), jnp.int32),
                pltpu.VMEM((nu * part // 128, cold_rows, 128), BF16),
                pltpu.VMEM((CH, nu, ROWS, rank), BF16),
                pltpu.VMEM((CH, nu, ROWS, rank), BF16),
                pltpu.VMEM((rank // 128, hot_rows, 128), F32),
                pltpu.VMEM((rank // 128, nu * ROWS, 128), F32),
                pltpu.VMEM((nblk, rank), F32),
                pltpu.VMEM((nblk, slots), BF16),
                pltpu.VMEM((slots, nblk), BF16),
                pltpu.VMEM((hp, rank), BF16),
                pltpu.VMEM((IB * HB, nblk), F32),
                pltpu.VMEM((rank, rank), F32),
                pltpu.VMEM((nblk, rank), F32),
                pltpu.VMEM((rank // 128, nu * ROWS, 128), F32),
                pltpu.VMEM((CH, nu, ROWS, rank), BF16),
                pltpu.VMEM((CH, nu, ROWS, rank), BF16),
                pltpu.VMEM((ni, udev, rank), F32),
                pltpu.VMEM((ni, udev, rank), BF16),
                pltpu.VMEM((ni, udev, rank), BF16),
                pltpu.VMEM((ni, udev, nblk), BF16),
                pltpu.VMEM((CH, 2, 2 * (hot_rows // IB), rank), BF16),
                pltpu.VMEM((2, ni, 2 * (hot_rows // IB), rank), BF16),
                pltpu.VMEM((ni, rank // ni, rank), BF16),
                pltpu.VMEM((ni, rank // ni, rank), BF16),
                pltpu.VMEM((nu, 1, rank), F32),
                pltpu.VMEM((nu, 1, rank), F32),
                pltpu.VMEM((2 * rank // 128, nu, 128), F32),
                pltpu.VMEM((nu, 1, 2 * rank), F32),
                pltpu.VMEM((nu, 1, 2 * rank), F32),
                pltpu.VMEM((ni, nu, 1, rank), F32),
                pltpu.VMEM((rank, rank), F32),
                pltpu.SemaphoreType.DMA((9 + 2 * CH, 2)),
            ],
            compiler_params=pltpu.CompilerParams(
                collective_id=0, has_side_effects=True, vmem_limit_bytes=56 * 1024 * 1024
            ),
        )(
            user_factor,
            hot_factor,
            cold_factor,
            hour_factor,
            block_user,
            block_slot,
            block_hour,
            block_count,
            need_rows,
            observed,
        )
        shapes = [jax.ShapeDtypeStruct(r.shape, r.dtype) for r in results]
        anywhere = pl.BlockSpec(memory_space=pl.ANY)
        return pl.pallas_call(
            keep,
            out_shape=shapes,
            in_specs=[anywhere] * 4,
            out_specs=[anywhere] * 4,
            scratch_shapes=[pltpu.VMEM(r.shape, r.dtype) for r in results]
            + [pltpu.SemaphoreType.DMA((4, 2))],
        )(*results)

    in_specs = (
        P("users", None),
        P(),
        P(("users", "items"), None),
        P(),
        P(("users", "items"), None),
        P(("users", "items"), None),
        P(("users", "items"), None),
        P(("users", "items")),
        P(("users", "items"), None, None),
        P(("users", "items"), None, None),
    )
    out_specs = (
        P(("users", "items"), None),
        P(("users", "items"), None),
        P(("users", "items"), None),
        P(),
    )
    return jax.shard_map(body, mesh=mesh, in_specs=in_specs, out_specs=out_specs, check_vma=False)
```
